32 devices in a mesh: half: 2 (over y), row: 4 (over z), col: 4 (over x, core).
Axes of the slice: x: 2, y: 2, z: 4, core: 2. Of those that a mesh axis runs over, the one named last changes fastest.
Arguments:
- children: bfloat16 [2, 512, 512, 512], P('half', 'row', 'col'), may hold values from -0.01171875 to 0.01171875
- operators: bfloat16 [2, 2, 4, 512, 512], P('half'), may hold values from -1 to 1
- term_site: int32 [2, 5, 2], P('half'), may hold values from 0 to 3
- term_leg: int32 [2, 5], P('half'), may hold values from 0 to 2
- parent: bfloat16 [512, 512, 512], P(('half', 'row', 'col')), may hold values from -6 to 6
Outputs:
- updated: bfloat16 [512, 512, 512], P(('half', 'row', 'col'))
The draws below stay inside these ranges and needn't reach their ends.
Inputs may be any that keep to these rules, and one draw needn't show every extreme that they name: `term_site`: a site index into the child's operator table of 4 entries. `term_leg`: 0: the term acts on the first leg only, 1: on the second leg only, 2: on both.
All inputs are finite; a program needn't handle non-finite values.
Results may differ from the reference program's by a relative error of at most 0.0064.
Values may be sent and summed in bfloat16 or wider, within the bound.
A program may use at most 320 MiB of HBM per device.

```python
import jax
import jax.numpy as jnp
from jax import lax

B = 512
C = 512
TERMS = 5
SITES = 4


def touch_ends(entries, stream_key, least, high):
    longest = entries.shape.index(max(entries.shape))
    spots = []
    for shift in (0, 1):
        where = [jax.random.randint(jax.random.fold_in(stream_key, axis), (), 0, length) for axis, length in enumerate(entries.shape)]
        where[longest] = (where[longest] + shift) % entries.shape[longest]
        spots.append(tuple(where))
    return entries.at[spots[0]].set(least).at[spots[1]].set(high)


def block_levels(own_key, dims, cuts, least, top_value):
    gain = 1.0
    for dim, parts in cuts:
        draws = jax.random.uniform(jax.random.fold_in(jax.random.fold_in(own_key, 6), dim), (parts,), jnp.float32, least / len(cuts), top_value / len(cuts))
        gain = gain * jnp.repeat(jnp.exp(draws), dims[dim] // parts).reshape((-1,) + (1,) * (len(dims) - 1 - dim))
    return gain


def scatter_about(rng, shape, deviation, most, cuts=(), kind=jnp.bfloat16):
    array = jax.random.normal(rng, shape, jnp.float32) * deviation
    if len(cuts) > 0:
        array = block_levels(rng, shape, cuts, -0.22, 0.18) * array
    return jnp.clip(array, min=-most, max=most).astype(kind)


def setup_inputs(seed: int = 0) -> dict:
    splits = jax.random.split(jax.random.key(seed), 6)
    return {
        "children": scatter_about(splits[0], (2, B, B, B), (B * B) ** -0.5, 0.01171875, ((0, 2), (1, 4), (2, 4))),
        "operators": scatter_about(splits[1], (2, 2, SITES, B, B), (B // 16) ** -0.5, 1.0, ((0, 2),)),
        "term_site": touch_ends(jax.random.randint(splits[2], (2, TERMS, 2), 0, SITES), jax.random.fold_in(splits[2], 1), 0, SITES - 1).astype(jnp.int32),
        "term_leg": touch_ends(jax.random.randint(splits[3], (2, TERMS), 0, 3), jax.random.fold_in(splits[3], 1), 0, 2).astype(jnp.int32),
        "parent": scatter_about(splits[4], (C, B, B), 1.0, 6.0, ((0, 32),)),
    }


def apply_terms(block, table, site_ids, leg_codes):
    identity = jnp.eye(B, dtype=block.dtype)
    accumulated = jnp.zeros(block.shape, jnp.float32)
    for term in range(TERMS):
        left_op = jnp.where(leg_codes[term] != 1, table[0, site_ids[term, 0]], identity)
        right_op = jnp.where(leg_codes[term] != 0, table[1, site_ids[term, 1]], identity)
        inner = jnp.einsum('aik,jk->aij', block.astype(jnp.float32), right_op.astype(jnp.float32)).astype(jnp.bfloat16)
        accumulated = accumulated + jnp.einsum('ik,akj->aij', left_op.astype(jnp.float32), inner.astype(jnp.float32))
    return accumulated.astype(jnp.bfloat16)


def environment_of(child, table, site_ids, leg_codes):
    group = min(64, B)
    blocks = child.reshape(B // group, group, B, B)
    summed = lax.map(lambda piece: apply_terms(piece, table, site_ids, leg_codes), blocks)
    flat_child = child.reshape(B, B * B)
    flat_summed = summed.reshape(B, B * B)
    product = lax.dot_general(flat_child, flat_summed, (((1,), (1,)), ((), ())), preferred_element_type=jnp.float32)
    return product.astype(jnp.bfloat16)


def reference(children, operators, term_site, term_leg, parent):
    left_env = environment_of(children[0], operators[0], term_site[0], term_leg[0])
    right_env = environment_of(children[1], operators[1], term_site[1], term_leg[1])
    parent_wide = parent.astype(jnp.float32)
    first = jnp.einsum('ak,ckb->cab', left_env.astype(jnp.float32), parent_wide)
    second = jnp.einsum('bk,cak->cab', right_env.astype(jnp.float32), parent_wide)
    return (first + second).astype(jnp.bfloat16)
```

```python
import functools

import jax
import jax.numpy as jnp
from jax import lax
from jax.experimental import pallas as pl
from jax.experimental.pallas import tpu as pltpu
from jax.sharding import PartitionSpec as P


def terms_kernel(pieces, batch, groups, flags_ref, *refs):
    piece_refs = refs[:pieces]
    left_ref, right_ref = refs[pieces], refs[pieces + 1]
    out_refs = refs[pieces + 2 : 2 * pieces + 2]
    acc_ref = refs[-1]
    rows = piece_refs[0].shape[1]
    for item in range(batch):
        acc_ref[...] = jnp.zeros_like(acc_ref)

        @pl.when(flags_ref[groups] > 0)
        def _():
            block = jnp.concatenate([ref[item] for ref in piece_refs], axis=0)
            acc_ref[...] = jnp.dot(block, right_ref[groups], preferred_element_type=jnp.float32)

        for group in range(groups):

            @pl.when(flags_ref[group] > 0)
            def _():
                block = jnp.concatenate([ref[item] for ref in piece_refs], axis=0)
                inner = jnp.dot(block, right_ref[group], preferred_element_type=jnp.float32)
                acc_ref[...] += jnp.dot(
                    left_ref[group], inner.astype(jnp.bfloat16), preferred_element_type=jnp.float32
                )

        for place in range(pieces):
            out_refs[place][item] = acc_ref[place * rows : (place + 1) * rows, :].astype(jnp.bfloat16)


def apply_terms(flags, blocks, left_ops, right_ops):
    pieces = len(blocks)
    count, rows, bond = blocks[0].shape
    groups = left_ops.shape[0]
    batch = 2 if count % 2 == 0 else 1
    piece_spec = pl.BlockSpec((batch, rows, bond), lambda a, f: (a, 0, 0))
    flops = 2 * (2 * groups + 1) * count * bond**3
    moved = 4 * count * bond * bond
    return pl.pallas_call(
        functools.partial(terms_kernel, pieces, batch, groups),
        out_shape=[jax.ShapeDtypeStruct((count, rows, bond), jnp.bfloat16)] * pieces,
        grid_spec=pltpu.PrefetchScalarGridSpec(
            num_scalar_prefetch=1,
            grid=(count // batch,),
            in_specs=[piece_spec] * pieces
            + [
                pl.BlockSpec(left_ops.shape, lambda a, f: (0, 0, 0)),
                pl.BlockSpec(right_ops.shape, lambda a, f: (0, 0, 0)),
            ],
            out_specs=[piece_spec] * pieces,
            scratch_shapes=[pltpu.VMEM((bond, bond), jnp.float32)],
        ),
        compiler_params=pltpu.CompilerParams(dimension_semantics=("arbitrary",)),
        cost_estimate=pl.CostEstimate(flops=flops, bytes_accessed=moved, transcendentals=0),
        name="apply_terms",
    )(flags, *blocks, left_ops, right_ops)


def on_device(rows, cols, children, operators, term_site, term_leg, parent):
    child = children[0]
    tops, firsts, bond = child.shape
    row = lax.axis_index("row")
    col = lax.axis_index("col")
    row_order = jnp.arange(rows) ^ row
    col_order = jnp.arange(cols) ^ col
    mine = tops // cols
    share = firsts // rows
    chunks = 4 if mine % 4 == 0 else 1
    step = mine // chunks

    def swap(value, axis, size, offset):
        if offset == 0:
            return value
        return lax.ppermute(value, axis, [(k, k ^ offset) for k in range(size)])

    table = operators[0].astype(jnp.float32)
    site_ids, leg_codes = term_site[0], term_leg[0]
    sites = table.shape[1]
    left_group = jnp.where(leg_codes != 1, site_ids[:, 0], sites)
    right_pick = jnp.where(leg_codes != 0, site_ids[:, 1], sites)
    in_group = (left_group[None, :] == jnp.arange(sites + 1)[:, None]).astype(jnp.float32)
    of_right = (right_pick[:, None] == jnp.arange(sites + 1)[None, :]).astype(jnp.float32)
    counts = jnp.sum(in_group[:, :, None] * of_right[None, :, :], axis=1)
    flags = (jnp.sum(counts, axis=1) > 0).astype(jnp.int32)
    turned = jnp.swapaxes(table[1], 1, 2)
    weights = counts[:, :sites, None, None] * turned[None]
    right_ops = jnp.sum(weights, axis=1) + counts[:, sites, None, None] * jnp.eye(bond, dtype=jnp.float32)
    right_ops = right_ops.astype(jnp.bfloat16)
    left_ops = operators[0, 0].reshape(sites, cols, firsts, cols, firsts)
    left_ops = jnp.take(jnp.take(left_ops, col_order, axis=1), col_order, axis=3)
    left_ops = left_ops.reshape(sites, bond, bond)

    entering = []
    for chunk in range(chunks):
        pieces = []
        for offset in range(cols):
            start = (col ^ offset) * mine + chunk * step
            piece = lax.dynamic_slice_in_dim(child, start, step, axis=0)
            pieces.append(swap(piece, "col", cols, offset))
        entering.append(pieces)

    flat_child = []
    for offset in range(rows):
        part = lax.dynamic_slice_in_dim(child, (row ^ offset) * share, share, axis=1)
        flat_child.append(swap(part.reshape(tops, share * bond), "row", rows, offset))
    flat_child = jnp.concatenate(flat_child, axis=0)

    columns = []
    for chunk in range(chunks):
        summed = apply_terms(flags, entering[chunk], left_ops, right_ops)
        summed = [swap(summed[offset], "col", cols, offset) for offset in range(cols)]
        for offset in range(rows):
            start = (row ^ offset) * share
            part = jnp.concatenate(
                [lax.dynamic_slice_in_dim(piece, start, share, axis=1) for piece in summed], axis=0
            )
            part = swap(part.reshape(cols * step, share * bond), "row", rows, offset)
            columns.append(
                lax.dot_general(
                    flat_child, part, (((1,), (1,)), ((), ())), preferred_element_type=jnp.float32
                )
            )
    partial = jnp.concatenate(columns, axis=1).reshape(rows, tops, chunks, rows, cols, step)
    partial = jnp.take(partial, row_order, axis=0)
    partial = jnp.take(partial, row_order, axis=3)
    partial = jnp.take(partial, col_order, axis=4)
    partial = jnp.transpose(partial, (0, 1, 3, 4, 2, 5)).reshape(bond, bond)

    slab = lax.psum_scatter(partial, ("row", "col"), scatter_dimension=0, tiled=True)
    envs = lax.all_gather(slab.astype(jnp.bfloat16), ("half", "row", "col"), axis=0, tiled=True)
    first = jnp.einsum("ak,ckb->cab", envs[:bond], parent, preferred_element_type=jnp.float32)
    second = jnp.einsum("bk,cak->cab", envs[bond:], parent, preferred_element_type=jnp.float32)
    return (first + second).astype(jnp.bfloat16)


def solution(mesh):
    placed = (
        P("half", "row", "col", None),
        P("half", None, None, None, None),
        P("half", None, None),
        P("half", None),
        P(("half", "row", "col"), None, None),
    )
    return jax.shard_map(
        functools.partial(on_device, mesh.shape["row"], mesh.shape["col"]),
        mesh=mesh,
        in_specs=placed,
        out_specs=P(("half", "row", "col"), None, None),
        check_vma=False,
    )
```
